32 devices in a mesh: groups: 1, rows: 16 (over z, y, core), heads: 2 (over x).
Axes of the slice: x: 2, y: 2, z: 4, core: 2. Of those that a mesh axis runs over, the one named last changes fastest.
Arguments:
- queries: bfloat16 [2048, 8192], P(('groups', 'rows'), 'heads'), may hold values from -40 to 40
- passages: bfloat16 [768, 1024], P(('groups', 'rows')), may hold values from -6 to 6
- enc_gain: bfloat16 [1024], replicated, may hold values from 0.099609375 to 1.8984375
- key_weight: bfloat16 [1024, 8192], P(None, 'heads'), may hold values from -0.1875 to 0.1875
- value_weight: bfloat16 [1024, 8192], P(None, 'heads'), may hold values from -0.1875 to 0.1875
- out_weight: bfloat16 [8192, 1024], P('heads'), may hold values from -0.125 to 0.125
- passage_length: int32 [3], P('groups'), may hold values from 64 to 256, as said below
Outputs:
- cross_out: bfloat16 [2048, 1024], P(('groups', 'rows'))
The draws below stay inside these ranges and needn't reach their ends.
Inputs may be any that keep to these rules, and one draw needn't show every extreme that they name: `passage_length`: every passage has at least a quarter of its padded tokens; some passage is full and some has exactly 64 tokens.
All inputs are finite; a program needn't handle non-finite values.
Results may differ from the reference program's by a relative error of at most 0.012.
The reference program's roundings to bfloat16 on the way count: a program that leaves them out, or rounds other values in their place, can miss the bound.
Values may be sent and summed in bfloat16 or wider, within the bound.
A program may use at most 128 MiB of HBM per device.

```python
import jax
import jax.numpy as jnp
from jax import lax

D = 1024
HEADS = 64
DK = 128
PASS_LEN = 256
ENC = 768
DEC = 2048
PASSAGES = 3


def draw_queries(key, part):
    first = jax.random.fold_in(key, 11)
    shape = (DEC, HEADS * DK)
    base = jnp.clip(0.25 * jax.random.normal(first, shape, jnp.float32), -1.5, 1.5)
    return base.astype(jnp.bfloat16)


def draw_passage_length(key, part):
    first = jax.random.fold_in(key, 21)
    second = jax.random.fold_in(key, 22)
    lowest_len = PASS_LEN // 4
    base = jax.random.randint(first, (PASSAGES,), lowest_len, PASS_LEN + 1)
    order = jax.random.permutation(second, PASSAGES)
    base = base.at[order[0]].set(PASS_LEN)
    base = base.at[order[1]].set(lowest_len)
    return base.astype(jnp.int32)


def steps_of(own_key, shape, pieces, low, top_value):
    factor_of, own = 1.0, jax.random.fold_in(own_key, 6)
    for position, shards_of in pieces:
        draws = jnp.exp(jax.random.uniform(jax.random.fold_in(own, position), (shards_of,), jnp.float32, low / len(pieces), top_value / len(pieces)))
        factor_of = factor_of * jnp.repeat(draws, shape[position] // shards_of).reshape([-1 if axis == position else 1 for axis in range(len(shape))])
    return factor_of


def scatter_about(key, dims, width, most, shards=(), held_as=jnp.bfloat16):
    loudness = steps_of(key, dims, shards, -0.22, 0.18) if shards else 1.0
    values = jax.random.normal(key, dims, jnp.float32) * width * loudness
    return jnp.minimum(jnp.maximum(values, -most), most).astype(held_as)


def setup_inputs(seed: int = 0, part: int = 0) -> dict:
    streams_of = jax.random.split(jax.random.key(seed), 8)
    part_splits = jax.random.split(jax.random.fold_in(streams_of[7], part), 8)
    return {
        "queries": draw_queries(jax.random.fold_in(jax.random.fold_in(streams_of[7], part), 71), part),
        "passages": scatter_about(part_splits[1], (ENC, D), 1.0, 6.0, ((0, 16),)),
        "enc_gain": jnp.clip(1.0 + 0.18 * jax.random.normal(streams_of[2], (D,), jnp.float32), 0.099609375, 1.8984375).astype(jnp.bfloat16),
        "key_weight": scatter_about(streams_of[3], (D, HEADS * DK), D ** -0.5, 0.1875, ((1, 2),)),
        "value_weight": scatter_about(streams_of[4], (D, HEADS * DK), D ** -0.5, 0.1875, ((1, 2),)),
        "out_weight": scatter_about(streams_of[5], (HEADS * DK, D), (HEADS * DK // 4) ** -0.5, 0.125, ((0, 2),)),
        "passage_length": draw_passage_length(jax.random.fold_in(jax.random.fold_in(streams_of[7], part), 71), part),
    }


LOWEST = -1e+30

def normalize(passages, enc_gain):
    wide = passages.astype(jnp.float32)
    mean_square = lax.optimization_barrier(jnp.mean(wide * wide, axis=-1, keepdims=True))
    return (wide * lax.rsqrt(mean_square + 1e-06) * enc_gain.astype(jnp.float32)).astype(jnp.bfloat16)

def reference(queries, passages, enc_gain, key_weight, value_weight, out_weight, passage_length):
    normed = normalize(passages, enc_gain)
    keys = jnp.dot(normed, key_weight, preferred_element_type=jnp.float32).astype(jnp.bfloat16)
    values = jnp.dot(normed, value_weight, preferred_element_type=jnp.float32).astype(jnp.bfloat16)
    positions = jnp.arange(ENC, dtype=jnp.int32)
    owner = positions // PASS_LEN
    valid = positions % PASS_LEN < passage_length[owner]
    key_heads = keys.reshape(ENC, HEADS, DK).transpose(1, 0, 2)
    value_heads = values.reshape(ENC, HEADS, DK).transpose(1, 0, 2)
    query_heads = queries.reshape(DEC, HEADS, DK).transpose(1, 0, 2)

    def one_head(operands):
        query_rows, key_rows, value_rows = operands
        scores = jnp.dot(query_rows, key_rows.T, preferred_element_type=jnp.float32)
        masked = jnp.where(valid[None, :], scores, LOWEST)
        top = lax.optimization_barrier(jnp.max(masked, axis=-1, keepdims=True))
        expo = jnp.where(valid[None, :], jnp.exp(scores - top), 0.0)
        denom = lax.optimization_barrier(jnp.sum(expo, axis=-1, keepdims=True))
        mixed = jnp.dot(expo.astype(jnp.bfloat16), value_rows, preferred_element_type=jnp.float32)
        return (mixed / denom).astype(jnp.bfloat16)
    attended = lax.map(one_head, (query_heads, key_heads, value_heads))
    attended = attended.transpose(1, 0, 2).reshape(DEC, HEADS * DK)
    return jnp.dot(attended, out_weight, preferred_element_type=jnp.float32).astype(jnp.bfloat16)
```

```python
import functools

import jax
import jax.numpy as jnp
from jax import lax
from jax.experimental import pallas as pl
from jax.experimental.pallas import tpu as pltpu
from jax.sharding import PartitionSpec as P

DK = 128
PASS_LEN = 256
SHORT_LEN = PASS_LEN // 4
LOWEST = -1e30
MESH = pl.DeviceIdType.MESH
LOADS = 4
GROUP = 2 * DK
OUT_CHUNK = 256


def flip(index, bits):
    bit = 1
    while bit <= bits:
        if bits & bit:
            index = index + bit - 2 * bit * ((index // bit) % 2)
        bit *= 2
    return index


def kernel(
    n_rows,
    n_heads,
    length_ref,
    queries_ref,
    passages_ref,
    gain_ref,
    key_ref,
    value_ref,
    outw_ref,
    out_ref,
    rows_all,
    normed,
    query_buf,
    key_w,
    value_w,
    out_w,
    keys,
    values,
    attended,
    core_send,
    core_recv,
    x_parts,
    local_sem,
    load_sem,
    z_send_sem,
    y_send_sem,
    x_send_sem,
    core_send_sem,
    main_recv,
    rest_recv,
    query_sem,
    out_core_sem,
    out_x_sem,
):
    block, width = passages_ref.shape
    dec, inner = queries_ref.shape
    half = inner // 2
    n_pass = length_ref.shape[0]
    n_z = n_rows // 4
    wide = width * 5 // 8
    narrow = width - wide

    me = lax.axis_index("rows")
    x = lax.axis_index("heads")
    core = me % 2
    y = (me // 2) % 2
    z = me // 4

    def row_of(z_, y_, c_):
        return (z_ * 2 + y_) * 2 + c_

    def at_row(r):
        return {"rows": r}

    partner = at_row(flip(me, 1))
    across_y = at_row(flip(me, 2))
    side = x % 2
    x_peers = [{"heads": flip(x, d)} for d in range(1, n_heads)]
    across_x = x_peers[0]

    def rows_at(r):
        return pl.ds(pl.multiple_of(r * block, 16), block)

    main_cols = pl.ds(pl.multiple_of(side * narrow, 128), wide)
    rest_cols = pl.ds(pl.multiple_of((1 - side) * wide, 128), narrow)
    give_cols = pl.ds(pl.multiple_of(side * wide, 128), narrow)

    own_rows = pltpu.make_async_copy(passages_ref, rows_all.at[rows_at(me)], local_sem.at[0])
    own_rows.start()
    mine = pl.ds(pl.multiple_of(core * half, 128), half)
    theirs = pl.ds(pl.multiple_of((1 - core) * half, 128), half)
    my_t = pl.ds(pl.multiple_of(core * dec, 128), dec)
    own_queries = pltpu.make_async_copy(
        queries_ref.at[:, mine], query_buf.at[my_t], local_sem.at[1]
    )
    own_queries.start()
    loads = []
    share = half // LOADS
    for part in range(LOADS):
        here = pl.ds(part * share, share)
        there = pl.ds(pl.multiple_of(core * half + part * share, 128), share)
        loads.append(
            (
                pltpu.make_async_copy(
                    key_ref.at[:, there], key_w.at[:, here], load_sem.at[0, part]
                ),
                pltpu.make_async_copy(
                    value_ref.at[:, there], value_w.at[:, here], load_sem.at[1, part]
                ),
                pltpu.make_async_copy(outw_ref.at[there], out_w.at[here], load_sem.at[2, part]),
            )
        )

    barrier = pltpu.get_barrier_semaphore()
    z_peers = [row_of(flip(z, d), y, core) for d in range(1, n_z)]
    peers = [at_row(r) for r in z_peers] + [across_y, partner] + x_peers
    for peer in peers:
        pl.semaphore_signal(barrier, inc=1, device_id=peer, device_id_type=MESH)
    pl.semaphore_wait(barrier, len(peers))

    sent = []

    def send(src, dst, send_sem, recv_sem, to):
        copy = pltpu.make_async_remote_copy(
            src_ref=src, dst_ref=dst, send_sem=send_sem, recv_sem=recv_sem,
            device_id=to, device_id_type=MESH,
        )
        copy.start()
        sent.append(copy)

    def send_block(r, cols, send_sem, recv_sem, to):
        view = rows_all.at[rows_at(r), cols]
        send(view, view, send_sem, recv_sem.at[r], to)

    def await_block(r, cols, recv_sem):
        view = rows_all.at[rows_at(r), cols]
        pltpu.make_async_copy(view, view, recv_sem.at[r]).wait()

    own_rows.wait()
    for d in range(1, n_z):
        send_block(me, main_cols, z_send_sem.at[d - 1], main_recv, at_row(z_peers[d - 1]))
    send_block(me, main_cols, y_send_sem.at[0], main_recv, across_y)
    send_block(me, main_cols, core_send_sem.at[0, 0], main_recv, partner)
    send_block(me, rest_cols, core_send_sem.at[1, 0], rest_recv, partner)
    send(
        queries_ref.at[:, theirs], query_buf.at[my_t], query_sem.at[0], query_sem.at[1], partner
    )
    for triple in loads:
        triple[0].start()
        triple[1].start()
    for triple in loads:
        triple[2].start()

    others = []
    from_y = row_of(z, 1 - y, core)
    order = [("y", from_y, 0)]
    for d in range(1, n_z):
        order.append(("z", z_peers[d - 1], d))
        order.append(("y", row_of(flip(z, d), 1 - y, core), d))
    for number, (kind, r, d) in enumerate(order):
        await_block(r, main_cols, main_recv)
        if kind == "z":
            send_block(r, main_cols, y_send_sem.at[d], main_recv, across_y)
        send_block(r, give_cols, x_send_sem.at[number], rest_recv, across_x)
        send_block(r, main_cols, core_send_sem.at[0, number + 1], main_recv, partner)
        others.append(r)
    for number, r in enumerate(others):
        await_block(r, rest_cols, rest_recv)
        send_block(r, rest_cols, core_send_sem.at[1, number + 1], rest_recv, partner)
    for r in [me] + others:
        await_block(flip(r, 1), main_cols, main_recv)
        await_block(flip(r, 1), rest_cols, rest_recv)

    lengths = [length_ref[p] for p in range(n_pass)]
    is_short = []
    open_still = jnp.int32(1)
    for p in range(n_pass):
        hit = open_still * (lengths[p] == SHORT_LEN).astype(jnp.int32)
        is_short.append(hit)
        open_still = open_still - hit
    passed = []
    seen = jnp.int32(0)
    for p in range(n_pass):
        seen = seen + is_short[p]
        passed.append(seen)
    gain = gain_ref[...].astype(jnp.float32)
    sizes = [PASS_LEN] * (n_pass - 1) + [SHORT_LEN]
    number = sum(sizes)
    offsets = lax.broadcasted_iota(jnp.int32, (1, number), 1)
    bias = jnp.zeros((1, number), jnp.float32)

    def lanes(flag, shape):
        return jnp.full(shape, flag, jnp.int32) == 1

    def normalize(start, raw):
        wide_rows = raw.astype(jnp.float32)
        mean_square = jnp.mean(wide_rows * wide_rows, axis=-1, keepdims=True)
        normed[start : start + raw.shape[0], :] = (
            wide_rows * lax.rsqrt(mean_square + 1e-06) * gain
        ).astype(jnp.bfloat16)

    step = SHORT_LEN
    for p in range(n_pass - 1):
        length = lengths[p] + passed[p] * (lengths[p + 1] - lengths[p])
        bad = (offsets >= p * PASS_LEN + length) & (offsets < (p + 1) * PASS_LEN)
        bias = jnp.where(bad, LOWEST, bias)
        moved = lanes(passed[p], (step, width))
        for row in range(p * PASS_LEN, (p + 1) * PASS_LEN, step):
            here = rows_all[row : row + step, :].astype(jnp.float32)
            after = rows_all[row + PASS_LEN : row + PASS_LEN + step, :].astype(jnp.float32)
            normalize(row, jnp.where(moved, after, here))
    last = rows_all[0:step, :].astype(jnp.float32)
    for p in range(1, n_pass):
        place = p * PASS_LEN
        here = rows_all[place : place + step, :].astype(jnp.float32)
        last = jnp.where(lanes(is_short[p], (step, width)), here, last)
    normalize((n_pass - 1) * PASS_LEN, last)

    for triple in loads:
        triple[0].wait()
        triple[1].wait()
    own_queries.wait()
    other_t = pl.ds(pl.multiple_of((1 - core) * dec, 128), dec)
    pltpu.make_async_copy(query_buf.at[other_t], query_buf.at[other_t], query_sem.at[1]).wait()

    groups = half // GROUP

    def project(g):
        cols = slice(g * GROUP, (g + 1) * GROUP)
        keys[g % 2] = jnp.dot(
            normed[...], key_w[:, cols], preferred_element_type=jnp.float32
        ).astype(jnp.bfloat16)
        values[g % 2] = jnp.dot(
            normed[...], value_w[:, cols], preferred_element_type=jnp.float32
        ).astype(jnp.bfloat16)

    def attend(g):
        for h in range(GROUP // DK):
            inside = slice(h * DK, (h + 1) * DK)
            cols = slice(g * GROUP + h * DK, g * GROUP + (h + 1) * DK)
            scores = lax.dot_general(
                query_buf[:, cols],
                keys[g % 2, :, inside],
                (((1,), (1,)), ((), ())),
                preferred_element_type=jnp.float32,
            )
            scores = scores + bias
            top = jnp.max(scores, axis=-1, keepdims=True)
            expo = jnp.exp(scores - top)
            denom = jnp.sum(expo, axis=-1, keepdims=True)
            mixed = jnp.dot(
                expo.astype(jnp.bfloat16),
                values[g % 2, :, inside],
                preferred_element_type=jnp.float32,
            )
            attended[:, cols] = (mixed / denom).astype(jnp.bfloat16)

    project(0)
    for g in range(groups):
        if g + 1 < groups:
            project(g + 1)
        attend(g)

    for triple in loads:
        triple[2].wait()
    chunks = width // OUT_CHUNK

    def chunk_of(j):
        return slice(j * OUT_CHUNK, (j + 1) * OUT_CHUNK)

    mine_parts = []
    for j in range(chunks):
        cols = chunk_of(j)
        core_send[:, cols] = jnp.dot(
            attended[other_t, :], out_w[:, cols], preferred_element_type=jnp.float32
        ).astype(jnp.bfloat16)
        send(
            core_send.at[:, cols], core_recv.at[:, cols], out_core_sem.at[0, j],
            out_core_sem.at[1, j], partner,
        )
        mine_parts.append(
            jnp.dot(attended[my_t, :], out_w[:, cols], preferred_element_type=jnp.float32)
        )
    for j in range(chunks):
        cols = chunk_of(j)
        view = core_recv.at[:, cols]
        pltpu.make_async_copy(view, view, out_core_sem.at[1, j]).wait()
        x_parts[x, :, cols] = (mine_parts[j] + core_recv[:, cols].astype(jnp.float32)).astype(
            jnp.bfloat16
        )
        view = x_parts.at[x, :, cols]
        for d, peer in enumerate(x_peers):
            send(view, view, out_x_sem.at[0, d, j], out_x_sem.at[1, d, j], peer)
    for j in range(chunks):
        cols = chunk_of(j)
        for d in range(1, n_heads):
            view = x_parts.at[flip(x, d), :, cols]
            pltpu.make_async_copy(view, view, out_x_sem.at[1, d - 1, j]).wait()
        total = x_parts[0, :, cols].astype(jnp.float32)
        for term in range(1, n_heads):
            total += x_parts[term, :, cols].astype(jnp.float32)
        out_ref[:, cols] = total.astype(jnp.bfloat16)
    for copy in sent:
        copy.wait_send()


def on_device(
    n_rows, n_heads, queries, passages, enc_gain, key_weight, value_weight, out_weight, passage_length
):
    dec, inner = queries.shape
    block, width = passages.shape
    half = inner // 2
    n_pass = passage_length.shape[0]
    number = (n_pass - 1) * PASS_LEN + SHORT_LEN
    n_z = n_rows // 4
    same = n_rows // 2
    chunks = width // OUT_CHUNK
    bf16 = jnp.bfloat16
    dma = pltpu.SemaphoreType.DMA
    vmem = pl.BlockSpec(memory_space=pltpu.VMEM)
    anywhere = pl.BlockSpec(memory_space=pl.ANY)
    return pl.pallas_call(
        functools.partial(kernel, n_rows, n_heads),
        out_shape=jax.ShapeDtypeStruct((dec, width), bf16),
        in_specs=[
            pl.BlockSpec(memory_space=pltpu.SMEM),
            anywhere,
            anywhere,
            vmem,
            anywhere,
            anywhere,
            anywhere,
        ],
        out_specs=vmem,
        scratch_shapes=[
            pltpu.VMEM((n_rows * block, width), bf16),
            pltpu.VMEM((number, width), bf16),
            pltpu.VMEM((2 * dec, half), bf16),
            pltpu.VMEM((width, half), bf16),
            pltpu.VMEM((width, half), bf16),
            pltpu.VMEM((half, width), bf16),
            pltpu.VMEM((2, number, GROUP), bf16),
            pltpu.VMEM((2, number, GROUP), bf16),
            pltpu.VMEM((2 * dec, half), bf16),
            pltpu.VMEM((dec, width), bf16),
            pltpu.VMEM((dec, width), bf16),
            pltpu.VMEM((n_heads, dec, width), bf16),
            dma((2,)),
            dma((3, LOADS)),
            dma((n_z - 1,)),
            dma((n_z,)),
            dma((same,)),
            dma((2, same)),
            dma((n_rows,)),
            dma((n_rows,)),
            dma((2,)),
            dma((2, chunks)),
            dma((2, n_heads - 1, chunks)),
        ],
        compiler_params=pltpu.CompilerParams(
            collective_id=0, has_side_effects=True, vmem_limit_bytes=60 * 1024 * 1024
        ),
    )(
        passage_length,
        queries,
        passages,
        enc_gain.reshape(1, width),
        key_weight,
        value_weight,
        out_weight,
    )


def solution(mesh):
    return jax.shard_map(
        functools.partial(on_device, mesh.shape["rows"], mesh.shape["heads"]),
        mesh=mesh,
        in_specs=(
            P(("groups", "rows"), "heads"),
            P(("groups", "rows"), None),
            P(),
            P(None, "heads"),
            P(None, "heads"),
            P("heads", None),
            P("groups"),
        ),
        out_specs=P(("groups", "rows"), None),
        check_vma=False,
    )
```

```python
import functools

import jax
import jax.numpy as jnp
from jax import lax
from jax.experimental import pallas as pl
from jax.experimental.pallas import tpu as pltpu
from jax.sharding import PartitionSpec as P

DK = 128
PASS_LEN = 256
SHORT_LEN = PASS_LEN // 4
LOWEST = -1e30
MESH = pl.DeviceIdType.MESH
LOADS = 4
GROUP = 2 * DK
OUT_CHUNK = 256


def flip(index, bits):
    bit = 1
    while bit <= bits:
        if bits & bit:
            index = index + bit - 2 * bit * ((index // bit) % 2)
        bit *= 2
    return index


def kernel(
    n_rows,
    n_heads,
    length_ref,
    queries_ref,
    passages_ref,
    gain_ref,
    key_ref,
    value_ref,
    outw_ref,
    out_ref,
    rows_all,
    norm_all,
    normed,
    query_buf,
    key_w,
    value_w,
    out_w,
    keys,
    values,
    attended,
    core_send,
    core_recv,
    own_part,
    x_parts,
    local_sem,
    load_sem,
    z_send_sem,
    y_send_sem,
    x_send_sem,
    core_send_sem,
    main_recv,
    rest_recv,
    query_sem,
    out_core_sem,
    out_x_sem,
):
    block, width = passages_ref.shape
    dec, inner = queries_ref.shape
    half = inner // 2
    n_pass = length_ref.shape[0]
    n_z = n_rows // 4
    wide = width * 5 // 8
    narrow = width - wide

    me = lax.axis_index("rows")
    x = lax.axis_index("heads")
    core = me % 2
    y = (me // 2) % 2
    z = me // 4

    def row_of(z_, y_, c_):
        return (z_ * 2 + y_) * 2 + c_

    def at_row(r):
        return {"rows": r}

    partner = at_row(flip(me, 1))
    across_y = at_row(flip(me, 2))
    side = x % 2
    x_peers = [{"heads": flip(x, d)} for d in range(1, n_heads)]
    across_x = x_peers[0]

    def rows_at(r):
        return pl.ds(pl.multiple_of(r * block, 16), block)

    main_cols = pl.ds(pl.multiple_of(side * narrow, 128), wide)
    rest_cols = pl.ds(pl.multiple_of((1 - side) * wide, 128), narrow)
    give_cols = pl.ds(pl.multiple_of(side * wide, 128), narrow)

    own_rows = pltpu.make_async_copy(passages_ref, rows_all.at[rows_at(me)], local_sem.at[0])
    own_rows.start()
    mine = pl.ds(pl.multiple_of(core * half, 128), half)
    theirs = pl.ds(pl.multiple_of((1 - core) * half, 128), half)
    my_t = pl.ds(pl.multiple_of(core * dec, 128), dec)
    own_queries = pltpu.make_async_copy(
        queries_ref.at[:, mine], query_buf.at[my_t], local_sem.at[1]
    )
    own_queries.start()
    loads = []
    share = half // LOADS
    for part in range(LOADS):
        here = pl.ds(part * share, share)
        there = pl.ds(pl.multiple_of(core * half + part * share, 128), share)
        loads.append(
            (
                pltpu.make_async_copy(
                    key_ref.at[:, there], key_w.at[:, here], load_sem.at[0, part]
                ),
                pltpu.make_async_copy(
                    value_ref.at[:, there], value_w.at[:, here], load_sem.at[1, part]
                ),
                pltpu.make_async_copy(outw_ref.at[there], out_w.at[here], load_sem.at[2, part]),
            )
        )

    barrier = pltpu.get_barrier_semaphore()
    z_peers = [row_of(flip(z, d), y, core) for d in range(1, n_z)]
    peers = [at_row(r) for r in z_peers] + [across_y, partner] + x_peers
    for peer in peers:
        pl.semaphore_signal(barrier, inc=1, device_id=peer, device_id_type=MESH)
    pl.semaphore_wait(barrier, len(peers))

    sent = []

    def send(src, dst, send_sem, recv_sem, to):
        copy = pltpu.make_async_remote_copy(
            src_ref=src, dst_ref=dst, send_sem=send_sem, recv_sem=recv_sem,
            device_id=to, device_id_type=MESH,
        )
        copy.start()
        sent.append(copy)

    def send_block(r, cols, send_sem, recv_sem, to):
        view = rows_all.at[rows_at(r), cols]
        send(view, view, send_sem, recv_sem.at[r], to)

    def await_block(r, cols, recv_sem):
        view = rows_all.at[rows_at(r), cols]
        pltpu.make_async_copy(view, view, recv_sem.at[r]).wait()

    def send_own(cols, send_sem, recv_sem, to):
        send(
            passages_ref.at[:, cols], rows_all.at[rows_at(me), cols], send_sem, recv_sem.at[me], to
        )

    for d in range(1, n_z):
        send_own(main_cols, z_send_sem.at[d - 1], main_recv, at_row(z_peers[d - 1]))
    send_own(main_cols, y_send_sem.at[0], main_recv, across_y)
    send_own(main_cols, core_send_sem.at[0, 0], main_recv, partner)
    send_own(rest_cols, core_send_sem.at[1, 0], rest_recv, partner)
    send(
        queries_ref.at[:, theirs], query_buf.at[my_t], query_sem.at[0], query_sem.at[1], partner
    )
    for triple in loads:
        triple[0].start()
        triple[1].start()
    for triple in loads:
        triple[2].start()

    others = []
    from_y = row_of(z, 1 - y, core)
    order = [("y", from_y, 0)]
    for d in range(1, n_z):
        order.append(("z", z_peers[d - 1], d))
        if d > 1:
            order.append(("y", row_of(flip(z, d - 1), 1 - y, core), d - 1))
    order.append(("y", row_of(flip(z, n_z - 1), 1 - y, core), n_z - 1))
    for number, (kind, r, d) in enumerate(order):
        await_block(r, main_cols, main_recv)
        if kind == "z":
            send_block(r, main_cols, y_send_sem.at[d], main_recv, across_y)
        send_block(r, give_cols, x_send_sem.at[number], rest_recv, across_x)
        send_block(r, main_cols, core_send_sem.at[0, number + 1], main_recv, partner)
        others.append(r)
    gain = gain_ref[...].astype(jnp.float32).reshape(1, width)

    def normalize(r):
        wide_rows = rows_all[rows_at(r), :].astype(jnp.float32)
        mean_square = jnp.mean(wide_rows * wide_rows, axis=-1, keepdims=True)
        norm_all[rows_at(r), :] = (
            wide_rows * lax.rsqrt(mean_square + 1e-06) * gain
        ).astype(jnp.bfloat16)

    def normalize_partner(r):
        await_block(flip(r, 1), main_cols, main_recv)
        await_block(flip(r, 1), rest_cols, rest_recv)
        normalize(flip(r, 1))

    own_rows.wait()
    normalize(me)
    normalize_partner(me)
    for number, r in enumerate(others):
        await_block(r, rest_cols, rest_recv)
        send_block(r, rest_cols, core_send_sem.at[1, number + 1], rest_recv, partner)
        normalize(r)
        if number:
            normalize_partner(others[number - 1])
    normalize_partner(others[-1])

    lengths = [length_ref[p] for p in range(n_pass)]
    is_short = []
    open_still = jnp.int32(1)
    for p in range(n_pass):
        hit = open_still * (lengths[p] == SHORT_LEN).astype(jnp.int32)
        is_short.append(hit)
        open_still = open_still - hit
    passed = []
    seen = jnp.int32(0)
    for p in range(n_pass):
        seen = seen + is_short[p]
        passed.append(seen)
    sizes = [PASS_LEN] * (n_pass - 1) + [SHORT_LEN]
    number = sum(sizes)
    offsets = lax.broadcasted_iota(jnp.int32, (1, number), 1)
    bias = jnp.zeros((1, number), jnp.float32)

    def lanes(flag, shape):
        return jnp.full(shape, flag, jnp.int32) == 1

    step = SHORT_LEN
    for p in range(n_pass - 1):
        length = lengths[p] + passed[p] * (lengths[p + 1] - lengths[p])
        bad = (offsets >= p * PASS_LEN + length) & (offsets < (p + 1) * PASS_LEN)
        bias = jnp.where(bad, LOWEST, bias)
        moved = lanes(passed[p], (step, width))
        for row in range(p * PASS_LEN, (p + 1) * PASS_LEN, step):
            here = norm_all[row : row + step, :].astype(jnp.float32)
            after = norm_all[row + PASS_LEN : row + PASS_LEN + step, :].astype(jnp.float32)
            normed[row : row + step, :] = jnp.where(moved, after, here).astype(jnp.bfloat16)
    last = norm_all[0:step, :].astype(jnp.float32)
    for p in range(1, n_pass):
        place = p * PASS_LEN
        here = norm_all[place : place + step, :].astype(jnp.float32)
        last = jnp.where(lanes(is_short[p], (step, width)), here, last)
    normed[number - step : number, :] = last.astype(jnp.bfloat16)

    for triple in loads:
        triple[0].wait()
        triple[1].wait()
    own_queries.wait()
    other_t = pl.ds(pl.multiple_of((1 - core) * dec, 128), dec)
    pltpu.make_async_copy(query_buf.at[other_t], query_buf.at[other_t], query_sem.at[1]).wait()

    groups = half // GROUP

    def project(g):
        cols = slice(g * GROUP, (g + 1) * GROUP)
        keys[:, cols] = jnp.dot(
            normed[...], key_w[:, cols], preferred_element_type=jnp.float32
        ).astype(jnp.bfloat16)
        values[:, cols] = jnp.dot(
            normed[...], value_w[:, cols], preferred_element_type=jnp.float32
        ).astype(jnp.bfloat16)

    def attend(g, low, high):
        size = high - low
        for h in range(GROUP // DK):
            cols = slice(g * GROUP + h * DK, g * GROUP + (h + 1) * DK)
            asked = jnp.concatenate(
                [query_buf[low:high, cols], query_buf[dec + low : dec + high, cols]], axis=0
            )
            scores = lax.dot_general(
                asked,
                keys[:, cols],
                (((1,), (1,)), ((), ())),
                preferred_element_type=jnp.float32,
            )
            scores = scores + bias
            top = jnp.max(scores, axis=-1, keepdims=True)
            expo = jnp.exp(scores - top)
            denom = jnp.sum(expo, axis=-1, keepdims=True)
            mixed = jnp.dot(
                expo.astype(jnp.bfloat16),
                values[:, cols],
                preferred_element_type=jnp.float32,
            )
            mixed = (mixed / denom).astype(jnp.bfloat16)
            attended[low:high, cols] = mixed[:size]
            attended[dec + low : dec + high, cols] = mixed[size:]

    chunks = width // OUT_CHUNK

    def chunk_of(j):
        return slice(j * OUT_CHUNK, (j + 1) * OUT_CHUNK)

    def core_rows(c, low, high):
        return pl.ds(pl.multiple_of(c * dec + low, 16), high - low)

    def to_core(n, low, high):
        rows = slice(low, high)
        for j in range(chunks):
            cols = chunk_of(j)
            core_send[rows, cols] = jnp.dot(
                attended[core_rows(1 - core, low, high), :],
                out_w[:, cols],
                preferred_element_type=jnp.float32,
            ).astype(jnp.bfloat16)
            send(
                core_send.at[rows, cols], core_recv.at[rows, cols], out_core_sem.at[0, n, j],
                out_core_sem.at[1, n, j], partner,
            )
        for j in range(chunks):
            cols = chunk_of(j)
            own_part[rows, cols] = jnp.dot(
                attended[core_rows(core, low, high), :],
                out_w[:, cols],
                preferred_element_type=jnp.float32,
            )

    def to_x(n, low, high):
        rows = slice(low, high)
        for j in range(chunks):
            cols = chunk_of(j)
            view = core_recv.at[rows, cols]
            pltpu.make_async_copy(view, view, out_core_sem.at[1, n, j]).wait()
            x_parts[x, rows, cols] = (
                own_part[rows, cols] + core_recv[rows, cols].astype(jnp.float32)
            ).astype(jnp.bfloat16)
            view = x_parts.at[x, rows, cols]
            for d, peer in enumerate(x_peers):
                send(view, view, out_x_sem.at[0, n, d, j], out_x_sem.at[1, n, d, j], peer)

    def finish(n, low, high):
        rows = slice(low, high)
        for j in range(chunks):
            cols = chunk_of(j)
            for d in range(1, n_heads):
                view = x_parts.at[flip(x, d), rows, cols]
                pltpu.make_async_copy(view, view, out_x_sem.at[1, n, d - 1, j]).wait()
            total = x_parts[0, rows, cols].astype(jnp.float32)
            for term in range(1, n_heads):
                total += x_parts[term, rows, cols].astype(jnp.float32)
            out_ref[rows, cols] = total.astype(jnp.bfloat16)

    project(0)
    for g in range(groups):
        if g + 1 < groups:
            project(g + 1)
        attend(g, 0, dec)
    for triple in loads:
        triple[2].wait()
    to_core(0, 0, dec)
    to_x(0, 0, dec)
    finish(0, 0, dec)
    for copy in sent:
        copy.wait_send()


def on_device(
    n_rows, n_heads, queries, passages, enc_gain, key_weight, value_weight, out_weight, passage_length
):
    dec, inner = queries.shape
    block, width = passages.shape
    half = inner // 2
    n_pass = passage_length.shape[0]
    number = (n_pass - 1) * PASS_LEN + SHORT_LEN
    n_z = n_rows // 4
    same = n_rows // 2
    chunks = width // OUT_CHUNK
    bf16 = jnp.bfloat16
    dma = pltpu.SemaphoreType.DMA
    vmem = pl.BlockSpec(memory_space=pltpu.VMEM)
    anywhere = pl.BlockSpec(memory_space=pl.ANY)
    return pl.pallas_call(
        functools.partial(kernel, n_rows, n_heads),
        out_shape=jax.ShapeDtypeStruct((dec, width), bf16),
        in_specs=[
            pl.BlockSpec(memory_space=pltpu.SMEM),
            anywhere,
            anywhere,
            vmem,
            anywhere,
            anywhere,
            anywhere,
        ],
        out_specs=vmem,
        scratch_shapes=[
            pltpu.VMEM((n_rows * block, width), bf16),
            pltpu.VMEM((n_rows * block, width), bf16),
            pltpu.VMEM((number, width), bf16),
            pltpu.VMEM((2 * dec, half), bf16),
            pltpu.VMEM((width, half), bf16),
            pltpu.VMEM((width, half), bf16),
            pltpu.VMEM((half, width), bf16),
            pltpu.VMEM((number, half), bf16),
            pltpu.VMEM((number, half), bf16),
            pltpu.VMEM((2 * dec, half), bf16),
            pltpu.VMEM((dec, width), bf16),
            pltpu.VMEM((dec, width), bf16),
            pltpu.VMEM((dec, width), jnp.float32),
            pltpu.VMEM((n_heads, dec, width), bf16),
            dma((2,)),
            dma((3, LOADS)),
            dma((n_z - 1,)),
            dma((n_z,)),
            dma((same,)),
            dma((2, same)),
            dma((n_rows,)),
            dma((n_rows,)),
            dma((2,)),
            dma((2, 1, chunks)),
            dma((2, 1, n_heads - 1, chunks)),
        ],
        compiler_params=pltpu.CompilerParams(
            collective_id=0, has_side_effects=True, vmem_limit_bytes=60 * 1024 * 1024
        ),
    )(
        passage_length,
        queries,
        passages,
        enc_gain,
        key_weight,
        value_weight,
        out_weight,
    )


def solution(mesh):
    return jax.shard_map(
        functools.partial(on_device, mesh.shape["rows"], mesh.shape["heads"]),
        mesh=mesh,
        in_specs=(
            P(("groups", "rows"), "heads"),
            P(("groups", "rows"), None),
            P(),
            P(None, "heads"),
            P(None, "heads"),
            P("heads", None),
            P("groups"),
        ),
        out_specs=P(("groups", "rows"), None),
        check_vma=False,
    )
```

```python
import functools

import jax
import jax.numpy as jnp
from jax import lax
from jax.experimental import pallas as pl
from jax.experimental.pallas import tpu as pltpu
from jax.sharding import PartitionSpec as P

DK = 128
PASS_LEN = 256
SHORT_LEN = PASS_LEN // 4
LOWEST = -1e30
MESH = pl.DeviceIdType.MESH
LOADS = 4
GROUP = 2 * DK
OUT_CHUNK = 512


def flip(index, bits):
    bit = 1
    while bit <= bits:
        if bits & bit:
            index = index + bit - 2 * bit * ((index // bit) % 2)
        bit *= 2
    return index


def kernel(
    n_rows,
    n_heads,
    length_ref,
    queries_ref,
    passages_ref,
    gain_ref,
    key_ref,
    value_ref,
    outw_ref,
    out_ref,
    rows_all,
    norm_all,
    normed,
    query_buf,
    key_w,
    value_w,
    out_w,
    keys,
    values,
    attended,
    core_send,
    core_recv,
    own_part,
    x_parts,
    local_sem,
    load_sem,
    z_send_sem,
    y_send_sem,
    x_send_sem,
    core_send_sem,
    main_recv,
    rest_recv,
    query_sem,
    out_core_sem,
    out_x_sem,
):
    block, width = passages_ref.shape
    dec, inner = queries_ref.shape
    half = inner // 2
    n_pass = length_ref.shape[0]
    n_z = n_rows // 4
    wide = width * 4 // 8
    narrow = width - wide

    me = lax.axis_index("rows")
    x = lax.axis_index("heads")
    core = me % 2
    y = (me // 2) % 2
    z = me // 4

    def row_of(z_, y_, c_):
        return (z_ * 2 + y_) * 2 + c_

    def at_row(r):
        return {"rows": r}

    partner = at_row(flip(me, 1))
    across_y = at_row(flip(me, 2))
    side = x % 2
    x_peers = [{"heads": flip(x, d)} for d in range(1, n_heads)]
    across_x = x_peers[0]

    def rows_at(r):
        return pl.ds(pl.multiple_of(r * block, 16), block)

    main_cols = pl.ds(pl.multiple_of(side * narrow, 128), wide)
    rest_cols = pl.ds(pl.multiple_of((1 - side) * wide, 128), narrow)
    give_cols = pl.ds(pl.multiple_of(side * wide, 128), narrow)

    own_rows = pltpu.make_async_copy(passages_ref, rows_all.at[rows_at(me)], local_sem.at[0])
    own_rows.start()
    mine = pl.ds(pl.multiple_of(core * half, 128), half)
    theirs = pl.ds(pl.multiple_of((1 - core) * half, 128), half)
    my_t = pl.ds(pl.multiple_of(core * dec, 128), dec)
    own_queries = pltpu.make_async_copy(
        queries_ref.at[:, mine], query_buf.at[my_t], local_sem.at[1]
    )
    own_queries.start()
    loads = []
    share = half // LOADS
    for part in range(LOADS):
        here = pl.ds(part * share, share)
        there = pl.ds(pl.multiple_of(core * half + part * share, 128), share)
        loads.append(
            (
                pltpu.make_async_copy(
                    key_ref.at[:, there], key_w.at[:, here], load_sem.at[0, part]
                ),
                pltpu.make_async_copy(
                    value_ref.at[:, there], value_w.at[:, here], load_sem.at[1, part]
                ),
                pltpu.make_async_copy(outw_ref.at[there], out_w.at[here], load_sem.at[2, part]),
            )
        )

    barrier = pltpu.get_barrier_semaphore()
    z_peers = [row_of(flip(z, d), y, core) for d in range(1, n_z)]
    peers = [at_row(r) for r in z_peers] + [across_y, partner] + x_peers
    for peer in peers:
        pl.semaphore_signal(barrier, inc=1, device_id=peer, device_id_type=MESH)
    pl.semaphore_wait(barrier, len(peers))

    sent = []

    def send(src, dst, send_sem, recv_sem, to):
        copy = pltpu.make_async_remote_copy(
            src_ref=src, dst_ref=dst, send_sem=send_sem, recv_sem=recv_sem,
            device_id=to, device_id_type=MESH,
        )
        copy.start()
        sent.append(copy)

    def send_block(r, cols, send_sem, recv_sem, to):
        view = rows_all.at[rows_at(r), cols]
        send(view, view, send_sem, recv_sem.at[r], to)

    def await_block(r, cols, recv_sem):
        view = rows_all.at[rows_at(r), cols]
        pltpu.make_async_copy(view, view, recv_sem.at[r]).wait()

    def send_own(cols, send_sem, recv_sem, to):
        send(
            passages_ref.at[:, cols], rows_all.at[rows_at(me), cols], send_sem, recv_sem.at[me], to
        )

    for d in range(1, n_z):
        send_own(main_cols, z_send_sem.at[d - 1], main_recv, at_row(z_peers[d - 1]))
    send_own(main_cols, y_send_sem.at[0], main_recv, across_y)
    send_own(main_cols, core_send_sem.at[0, 0], main_recv, partner)
    send_own(rest_cols, core_send_sem.at[1, 0], rest_recv, partner)
    send(
        queries_ref.at[:, theirs], query_buf.at[my_t], query_sem.at[0], query_sem.at[1], partner
    )
    for triple in loads:
        triple[0].start()
        triple[1].start()
    for triple in loads:
        triple[2].start()

    others = []
    from_y = row_of(z, 1 - y, core)
    order = [("y", from_y, 0)]
    for d in range(1, n_z):
        order.append(("z", z_peers[d - 1], d))
        if d > 1:
            order.append(("y", row_of(flip(z, d - 1), 1 - y, core), d - 1))
    order.append(("y", row_of(flip(z, n_z - 1), 1 - y, core), n_z - 1))
    for number, (kind, r, d) in enumerate(order):
        await_block(r, main_cols, main_recv)
        if kind == "z":
            send_block(r, main_cols, y_send_sem.at[d], main_recv, across_y)
        send_block(r, give_cols, x_send_sem.at[number], rest_recv, across_x)
        send_block(r, main_cols, core_send_sem.at[0, number + 1], main_recv, partner)
        others.append(r)
    gain = gain_ref[...].astype(jnp.float32).reshape(1, width)

    def normalize(r):
        wide_rows = rows_all[rows_at(r), :].astype(jnp.float32)
        mean_square = jnp.mean(wide_rows * wide_rows, axis=-1, keepdims=True)
        norm_all[rows_at(r), :] = (
            wide_rows * lax.rsqrt(mean_square + 1e-06) * gain
        ).astype(jnp.bfloat16)

    def normalize_partner(r):
        await_block(flip(r, 1), main_cols, main_recv)
        await_block(flip(r, 1), rest_cols, rest_recv)
        normalize(flip(r, 1))

    own_rows.wait()
    normalize(me)
    normalize_partner(me)
    for number, r in enumerate(others):
        await_block(r, rest_cols, rest_recv)
        send_block(r, rest_cols, core_send_sem.at[1, number + 1], rest_recv, partner)
        normalize(r)
        if number:
            normalize_partner(others[number - 1])
    normalize_partner(others[-1])

    lengths = [length_ref[p] for p in range(n_pass)]
    is_short = []
    open_still = jnp.int32(1)
    for p in range(n_pass):
        hit = open_still * (lengths[p] == SHORT_LEN).astype(jnp.int32)
        is_short.append(hit)
        open_still = open_still - hit
    passed = []
    seen = jnp.int32(0)
    for p in range(n_pass):
        seen = seen + is_short[p]
        passed.append(seen)
    sizes = [PASS_LEN] * (n_pass - 1) + [SHORT_LEN]
    number = sum(sizes)
    offsets = lax.broadcasted_iota(jnp.int32, (1, number), 1)
    bias = jnp.zeros((1, number), jnp.float32)

    def lanes(flag, shape):
        return jnp.full(shape, flag, jnp.int32) == 1

    step = SHORT_LEN
    for p in range(n_pass - 1):
        length = lengths[p] + passed[p] * (lengths[p + 1] - lengths[p])
        bad = (offsets >= p * PASS_LEN + length) & (offsets < (p + 1) * PASS_LEN)
        bias = jnp.where(bad, LOWEST, bias)
        moved = lanes(passed[p], (step, width))
        for row in range(p * PASS_LEN, (p + 1) * PASS_LEN, step):
            here = norm_all[row : row + step, :].astype(jnp.float32)
            after = norm_all[row + PASS_LEN : row + PASS_LEN + step, :].astype(jnp.float32)
            normed[row : row + step, :] = jnp.where(moved, after, here).astype(jnp.bfloat16)
    last = norm_all[0:step, :].astype(jnp.float32)
    for p in range(1, n_pass):
        place = p * PASS_LEN
        here = norm_all[place : place + step, :].astype(jnp.float32)
        last = jnp.where(lanes(is_short[p], (step, width)), here, last)
    normed[number - step : number, :] = last.astype(jnp.bfloat16)

    for triple in loads:
        triple[0].wait()
        triple[1].wait()
    own_queries.wait()
    other_t = pl.ds(pl.multiple_of((1 - core) * dec, 128), dec)
    pltpu.make_async_copy(query_buf.at[other_t], query_buf.at[other_t], query_sem.at[1]).wait()

    groups = half // GROUP

    def project(g):
        cols = slice(g * GROUP, (g + 1) * GROUP)
        keys[:, cols] = jnp.dot(
            normed[...], key_w[:, cols], preferred_element_type=jnp.float32
        ).astype(jnp.bfloat16)
        values[:, cols] = jnp.dot(
            normed[...], value_w[:, cols], preferred_element_type=jnp.float32
        ).astype(jnp.bfloat16)

    def attend(g, low, high):
        size = high - low
        for h in range(GROUP // DK):
            cols = slice(g * GROUP + h * DK, g * GROUP + (h + 1) * DK)
            asked = jnp.concatenate(
                [query_buf[low:high, cols], query_buf[dec + low : dec + high, cols]], axis=0
            )
            scores = lax.dot_general(
                asked,
                keys[:, cols],
                (((1,), (1,)), ((), ())),
                preferred_element_type=jnp.float32,
            )
            scores = scores + bias
            top = jnp.max(scores, axis=-1, keepdims=True)
            expo = jnp.exp(scores - top)
            denom = jnp.sum(expo, axis=-1, keepdims=True)
            mixed = jnp.dot(
                expo.astype(jnp.bfloat16),
                values[:, cols],
                preferred_element_type=jnp.float32,
            )
            mixed = (mixed / denom).astype(jnp.bfloat16)
            attended[low:high, cols] = mixed[:size]
            attended[dec + low : dec + high, cols] = mixed[size:]

    chunks = width // OUT_CHUNK

    def chunk_of(j):
        return slice(j * OUT_CHUNK, (j + 1) * OUT_CHUNK)

    def core_rows(c, low, high):
        return pl.ds(pl.multiple_of(c * dec + low, 16), high - low)

    def to_core(n, low, high):
        rows = slice(low, high)
        for j in range(chunks):
            cols = chunk_of(j)
            core_send[rows, cols] = jnp.dot(
                attended[core_rows(1 - core, low, high), :],
                out_w[:, cols],
                preferred_element_type=jnp.float32,
            ).astype(jnp.bfloat16)
            send(
                core_send.at[rows, cols], core_recv.at[rows, cols], out_core_sem.at[0, n, j],
                out_core_sem.at[1, n, j], partner,
            )
        for j in range(chunks):
            cols = chunk_of(j)
            own_part[rows, cols] = jnp.dot(
                attended[core_rows(core, low, high), :],
                out_w[:, cols],
                preferred_element_type=jnp.float32,
            )

    def to_x(n, low, high):
        rows = slice(low, high)
        for j in range(chunks):
            cols = chunk_of(j)
            view = core_recv.at[rows, cols]
            pltpu.make_async_copy(view, view, out_core_sem.at[1, n, j]).wait()
            x_parts[x, rows, cols] = (
                own_part[rows, cols] + core_recv[rows, cols].astype(jnp.float32)
            ).astype(jnp.bfloat16)
            view = x_parts.at[x, rows, cols]
            for d, peer in enumerate(x_peers):
                send(view, view, out_x_sem.at[0, n, d, j], out_x_sem.at[1, n, d, j], peer)

    def finish(n, low, high):
        rows = slice(low, high)
        for j in range(chunks):
            cols = chunk_of(j)
            for d in range(1, n_heads):
                view = x_parts.at[flip(x, d), rows, cols]
                pltpu.make_async_copy(view, view, out_x_sem.at[1, n, d - 1, j]).wait()
            total = x_parts[0, rows, cols].astype(jnp.float32)
            for term in range(1, n_heads):
                total += x_parts[term, rows, cols].astype(jnp.float32)
            out_ref[rows, cols] = total.astype(jnp.bfloat16)

    project(0)
    for g in range(groups):
        if g + 1 < groups:
            project(g + 1)
        attend(g, 0, dec)
    for triple in loads:
        triple[2].wait()
    to_core(0, 0, dec)
    to_x(0, 0, dec)
    finish(0, 0, dec)
    for copy in sent:
        copy.wait_send()


def on_device(
    n_rows, n_heads, queries, passages, enc_gain, key_weight, value_weight, out_weight, passage_length
):
    dec, inner = queries.shape
    block, width = passages.shape
    half = inner // 2
    n_pass = passage_length.shape[0]
    number = (n_pass - 1) * PASS_LEN + SHORT_LEN
    n_z = n_rows // 4
    same = n_rows // 2
    chunks = width // OUT_CHUNK
    bf16 = jnp.bfloat16
    dma = pltpu.SemaphoreType.DMA
    vmem = pl.BlockSpec(memory_space=pltpu.VMEM)
    anywhere = pl.BlockSpec(memory_space=pl.ANY)
    return pl.pallas_call(
        functools.partial(kernel, n_rows, n_heads),
        out_shape=jax.ShapeDtypeStruct((dec, width), bf16),
        in_specs=[
            pl.BlockSpec(memory_space=pltpu.SMEM),
            anywhere,
            anywhere,
            vmem,
            anywhere,
            anywhere,
            anywhere,
        ],
        out_specs=vmem,
        scratch_shapes=[
            pltpu.VMEM((n_rows * block, width), bf16),
            pltpu.VMEM((n_rows * block, width), bf16),
            pltpu.VMEM((number, width), bf16),
            pltpu.VMEM((2 * dec, half), bf16),
            pltpu.VMEM((width, half), bf16),
            pltpu.VMEM((width, half), bf16),
            pltpu.VMEM((half, width), bf16),
            pltpu.VMEM((number, half), bf16),
            pltpu.VMEM((number, half), bf16),
            pltpu.VMEM((2 * dec, half), bf16),
            pltpu.VMEM((dec, width), bf16),
            pltpu.VMEM((dec, width), bf16),
            pltpu.VMEM((dec, width), jnp.float32),
            pltpu.VMEM((n_heads, dec, width), bf16),
            dma((2,)),
            dma((3, LOADS)),
            dma((n_z - 1,)),
            dma((n_z,)),
            dma((same,)),
            dma((2, same)),
            dma((n_rows,)),
            dma((n_rows,)),
            dma((2,)),
            dma((2, 1, chunks)),
            dma((2, 1, n_heads - 1, chunks)),
        ],
        compiler_params=pltpu.CompilerParams(
            collective_id=0, has_side_effects=True, vmem_limit_bytes=60 * 1024 * 1024
        ),
    )(
        passage_length,
        queries,
        passages,
        enc_gain,
        key_weight,
        value_weight,
        out_weight,
    )


def solution(mesh):
    return jax.shard_map(
        functools.partial(on_device, mesh.shape["rows"], mesh.shape["heads"]),
        mesh=mesh,
        in_specs=(
            P(("groups", "rows"), "heads"),
            P(("groups", "rows"), None),
            P(),
            P(None, "heads"),
            P(None, "heads"),
            P("heads", None),
            P("groups"),
        ),
        out_specs=P(("groups", "rows"), None),
        check_vma=False,
    )
```
